512 devices in a mesh: vox: 32 (over x, z), smp: 16 (over y, core).
Axes of the slice: x: 4, y: 8, z: 8, core: 2. Of those that a mesh axis runs over, the one named last changes fastest.
Arguments:
- ensemble: float32 [4096, 128, 128], P('vox', 'smp'), may hold values from -6 to 6
- voxel_factor: float32 [4096, 128], P('vox'), may hold values from -6 to 6
- sample_factor: float32 [128, 128], P('smp'), may hold values from -6 to 6
- time_factor: float32 [128, 128], replicated, may hold values from -6 to 6
- weights: float32 [128], replicated, may hold values from 0.005 to 0.02
Outputs:
- voxel_result: float32 [4096, 128], P('vox')
- sample_result: float32 [128, 128], P('smp')
- time_result: float32 [128, 128], replicated
- scale_result: float32 [128], replicated
The draws below stay inside these ranges and needn't reach their ends.
All inputs are finite; a program needn't handle non-finite values. Where the reference program divides by a largest or mean magnitude, that divisor is 1e-20 or more.
Results may differ from the reference program's by a relative error of at most 0.0001.
Values sent between devices are 32-bit elements; how exact they have to be, the bound alone decides.
A program may use at most 64 MiB of HBM per device.

```python
import math
import jax
import jax.numpy as jnp
from jax import lax

VOX_DEV = 128
TIMES = 128
RANK = 128
SWEEPS = 1
VOXELS = 4096
SAMPLES = 128
N_VOX = 32


def levels(own_key, shape, pieces, low, high):
    gain, own = 1.0, jax.random.fold_in(own_key, 6)
    for dim, parts in pieces:
        steps = jnp.exp(jax.random.uniform(jax.random.fold_in(own, dim), (parts,), jnp.float32, low / len(pieces), high / len(pieces)))
        gain = gain * jnp.repeat(steps, shape[dim] // parts).reshape([-1 if axis == dim else 1 for axis in range(len(shape))])
    return gain


def bell_draw(rng, extent, scale, limit, shards=(), held_as=jnp.bfloat16):
    factor_of = levels(rng, extent, shards, -0.22, 0.18) if shards else 1.0
    drawn = jax.random.normal(rng, extent, jnp.float32) * scale * factor_of
    return jnp.minimum(jnp.maximum(drawn, -limit), limit).astype(held_as)


def setup_inputs(seed: int = 0) -> dict:
    key_list = jax.random.split(jax.random.key(seed), 6)
    ensemble = bell_draw(key_list[0], (VOXELS, SAMPLES, TIMES), 1.0, 6.0, ((0, 32), (1, 16)), jnp.float32)
    voxel_factor = bell_draw(key_list[1], (VOXELS, RANK), 1.0, 6.0, ((0, 32),), jnp.float32)
    sample_factor = bell_draw(key_list[2], (SAMPLES, RANK), 1.0, 6.0, ((0, 16),), jnp.float32)
    time_factor = bell_draw(key_list[3], (TIMES, RANK), 1.0, 6.0, (), jnp.float32)
    weights = jnp.clip(jnp.exp(jax.random.uniform(key_list[4], (RANK,), jnp.float32, math.log(0.005), math.log(0.02))), 0.005, 0.02)
    return dict(ensemble=ensemble, voxel_factor=voxel_factor, sample_factor=sample_factor, time_factor=time_factor, weights=weights)


HIGH = lax.Precision.HIGHEST

def descend(factor, terms, hadamard, weights):
    coupled = weights[:, None] * weights[None, :] * hadamard
    step_size = 1.0 / jnp.max(lax.optimization_barrier(jnp.sum(jnp.abs(coupled), axis=1)))
    product = jnp.dot(factor, coupled, precision=HIGH, preferred_element_type=jnp.float32)
    return factor - step_size * (product - terms * weights[None, :])

def rescale(moved, gram, row_count):
    scales = jnp.sqrt(jnp.diagonal(gram) / row_count + 1e-06)
    return (moved / scales[None, :], gram / (scales[:, None] * scales[None, :]), scales)

def reference(ensemble, voxel_factor, sample_factor, time_factor, weights):
    blocks = ensemble.reshape(N_VOX, VOX_DEV, SAMPLES, TIMES)
    gram_b = jnp.dot(sample_factor.T, sample_factor, precision=HIGH, preferred_element_type=jnp.float32)
    gram_c = jnp.dot(time_factor.T, time_factor, precision=HIGH, preferred_element_type=jnp.float32)
    for sweep_index in range(SWEEPS):
        current_b = sample_factor
        current_c = time_factor

        def voxel_block(block):
            contracted = jnp.einsum('ijk,kr->ijr', block, current_c, precision=HIGH)
            return jnp.einsum('ijr,jr->ir', contracted, current_b, precision=HIGH)
        terms_a = lax.map(voxel_block, blocks).reshape(VOXELS, RANK)
        moved = descend(voxel_factor, terms_a, gram_b * gram_c, weights)
        gram = jnp.dot(moved.T, moved, precision=HIGH, preferred_element_type=jnp.float32)
        voxel_factor, gram_a, scales = rescale(moved, gram, VOXELS)
        weights = weights * scales
        voxel_blocks = voxel_factor.reshape(N_VOX, VOX_DEV, RANK)

        def sample_block(pair):
            block, rows_a = pair
            contracted = jnp.einsum('ijk,kr->ijr', block, current_c, precision=HIGH)
            return jnp.einsum('ijr,ir->jr', contracted, rows_a, precision=HIGH)
        terms_b = lax.optimization_barrier(jnp.sum(lax.map(sample_block, (blocks, voxel_blocks)), axis=0))
        moved = descend(sample_factor, terms_b, gram_a * gram_c, weights)
        gram = jnp.dot(moved.T, moved, precision=HIGH, preferred_element_type=jnp.float32)
        sample_factor, gram_b, scales = rescale(moved, gram, SAMPLES)
        weights = weights * scales
        newer_b = sample_factor

        def time_block(pair):
            block, rows_a = pair
            paired = rows_a[:, None, :] * newer_b[None, :, :]
            return jnp.einsum('ijk,ijr->kr', block, paired, precision=HIGH)
        terms_c = lax.optimization_barrier(jnp.sum(lax.map(time_block, (blocks, voxel_blocks)), axis=0))
        moved = descend(time_factor, terms_c, gram_a * gram_b, weights)
        gram = jnp.dot(moved.T, moved, precision=HIGH, preferred_element_type=jnp.float32)
        time_factor, gram_c, scales = rescale(moved, gram, TIMES)
        weights = weights * scales
    return (voxel_factor, sample_factor, time_factor, weights)
```

```python
import functools

import jax
import jax.numpy as jnp
from jax import lax
from jax.experimental import pallas as pl
from jax.experimental.pallas import tpu as pltpu
from jax.sharding import PartitionSpec as P

MESH = pl.DeviceIdType.MESH
RANK = 128
X_CHIPS = 4

GATHER_B, SCATTER_A, GATHER_A, ALONG_X, ALONG_Z, GATHER_GRAM = range(6)
GATHER_MOVED_B, SCATTER_C, ALONG_X_C, ALONG_Z_C, GATHER_C = range(6, 11)
PHASES = 11


def split(value):
    high = value.astype(jnp.bfloat16)
    low = (value - high.astype(jnp.float32)).astype(jnp.bfloat16)
    return high, low


def left_operand(value):
    return jnp.concatenate(split(value), axis=1)


def right_operand(value):
    high, low = split(value)
    return jnp.concatenate(
        [jnp.concatenate([high, low], axis=1), jnp.concatenate([high, jnp.zeros_like(low)], axis=1)], axis=0
    )


def dot_split(left, right):
    both = jnp.dot(left, right, preferred_element_type=jnp.float32)
    half = both.shape[1] // 2
    return both[:, :half] + both[:, half:]


def dot3(left, right):
    return dot_split(left_operand(left), right_operand(right))


def step_of(coupled):
    sums = jnp.sum(jnp.abs(coupled), axis=0, keepdims=True)
    return 1.0 / jnp.max(sums, axis=1, keepdims=True)


def kernel(
    x_count, z_count, s_count,
    e_in, a_in, b_in, c_in, w_in,
    a_out, b_out, c_out, w_out,
    e_v, a_v, b_v, c_v, w_v,
    contracted, e_turned, turned, partial, partial_c,
    all_b, parts_a, all_a, along_x, along_z, all_gram,
    all_moved_b, parts_c, along_x_c, along_z_c, all_c,
    load_sem, send_sem, recv_sem,
):
    vox = lax.axis_index("vox")
    me = lax.axis_index("smp")
    x = vox // z_count
    z = vox % z_count
    rows_i = a_v.shape[0] * a_v.shape[1]
    rows_j = b_v.shape[0]

    loads = [
        pltpu.make_async_copy(src, dst, load_sem.at[n])
        for n, (src, dst) in enumerate(((c_in, c_v), (b_in, b_v), (e_in, e_v), (w_in, w_v), (a_in, a_v)))
    ]
    for load in loads:
        load.start()

    def smp_peer(d):
        return {"smp": lax.rem(me + d, s_count)}

    def x_peer(d):
        return {"vox": lax.rem(x + d, x_count) * z_count + z}

    def z_peer(d):
        return {"vox": x * z_count + lax.rem(z + d, z_count)}

    barrier = pltpu.get_barrier_semaphore()
    groups = ((smp_peer, s_count), (x_peer, x_count), (z_peer, z_count))
    for peer, count in groups:
        for d in range(1, count):
            pl.semaphore_signal(barrier, inc=1, device_id=peer(d), device_id_type=MESH)

    def copy(src, dst, phase, device):
        return pltpu.make_async_remote_copy(
            src_ref=src, dst_ref=dst, send_sem=send_sem.at[phase], recv_sem=recv_sem.at[phase],
            device_id=device, device_id_type=MESH,
        )

    def gather(buffer, index, peer, count, phase):
        for d in range(1, count):
            copy(buffer.at[index], buffer.at[index], phase, peer(d)).start()

    def scatter(source, buffer, phase):
        for d in range(1, s_count):
            p = lax.rem(me + d, s_count)
            copy(source.at[p], buffer.at[me], phase, {"smp": p}).start()
        buffer[me] = source[me]

    def arrived(buffer, phase, sem=recv_sem):
        others = buffer.at[pl.ds(0, buffer.shape[0] - 1)]
        pltpu.make_async_copy(others, others, sem.at[phase]).wait()

    def whole(buffer):
        return buffer[...].reshape(buffer.shape[0] * buffer.shape[1], RANK)

    loads[0].wait()
    c = c_v[...].reshape(RANK, RANK)
    c_right = right_operand(c)
    loads[1].wait()
    loads[2].wait()
    total = jnp.zeros((rows_i, RANK), jnp.float32)
    for j in range(rows_j):
        rows = e_v[pl.ds(j, rows_i, stride=rows_j), :]
        product = dot_split(left_operand(rows), c_right)
        contracted[j] = product
        total = total + product * b_v[j : j + 1, :]
    partial[...] = total.reshape(partial.shape)
    all_b[me] = b_v[...]

    pl.semaphore_wait(barrier, sum(count - 1 for _, count in groups))
    gather(all_b, me, smp_peer, s_count, GATHER_B)
    scatter(partial, parts_a, SCATTER_A)

    loads[3].wait()
    loads[4].wait()
    w = w_v[...]
    w_pairs = jnp.broadcast_to(w, (RANK, RANK)).T * w
    w_gram_c = w_pairs * dot3(c.T, c)
    for j in range(rows_j):
        e_turned[j] = left_operand(e_v[pl.ds(j, rows_i, stride=rows_j), :].T)
    arrived(all_b, GATHER_B)
    b_all = whole(all_b)
    samples = b_all.shape[0]
    gram_b = dot3(b_all.T, b_all)
    coupled = w_gram_c * gram_b
    step = step_of(coupled)
    a_own = a_v[me]
    base = a_own - step * dot3(a_own, coupled)
    gain = step * w

    arrived(parts_a, SCATTER_A)
    moved = base + gain * jnp.sum(parts_a[...], axis=0)
    all_a[me] = moved
    gather(all_a, me, smp_peer, s_count, GATHER_A)
    arrived(all_a, GATHER_A)

    moved_a = whole(all_a)
    turned[...] = moved_a.T.reshape(turned.shape)
    a_right = right_operand(moved_a)
    chunk = turned.shape[1]
    along_x[x, :chunk, :] = dot_split(left_operand(turned[me]), a_right)
    along_x[x, chunk:, :] = jnp.concatenate(
        [jnp.sum(contracted[j] * moved_a, axis=0, keepdims=True) for j in range(rows_j)], axis=0
    )
    gather(along_x, x, x_peer, x_count, ALONG_X)
    for j in range(rows_j // 2):
        contracted[j] = dot_split(e_turned[j], a_right)
    arrived(along_x, ALONG_X)
    along_z[z] = jnp.sum(along_x[...], axis=0)
    gather(along_z, z, z_peer, z_count, ALONG_Z)
    for j in range(rows_j // 2, rows_j):
        contracted[j] = dot_split(e_turned[j], a_right)
    b_own = b_v[...]
    b_left = left_operand(b_own)
    arrived(along_z, ALONG_Z)
    summed = jnp.sum(along_z[...], axis=0)
    all_gram[me] = summed[:chunk]
    gather(all_gram, me, smp_peer, s_count, GATHER_GRAM)
    terms_b = summed[chunk:] * w
    arrived(all_gram, GATHER_GRAM)

    gram_a = whole(all_gram)
    coupled = w_gram_c * gram_a
    step = step_of(coupled)
    moved_b = b_own - step * (dot_split(b_left, right_operand(coupled)) - terms_b)
    total = contracted[0] * moved_b[0:1, :]
    for j in range(1, rows_j):
        total = total + contracted[j] * moved_b[j : j + 1, :]
    partial_c[...] = total.reshape(partial_c.shape)
    scatter(partial_c, parts_c, SCATTER_C)
    all_moved_b[me] = moved_b
    gather(all_moved_b, me, smp_peer, s_count, GATHER_MOVED_B)

    diagonal = (
        lax.broadcasted_iota(jnp.int32, (RANK, RANK), 0) == lax.broadcasted_iota(jnp.int32, (RANK, RANK), 1)
    )

    def scales_of(gram, count):
        own = jnp.sum(jnp.where(diagonal, gram, 0.0), axis=0, keepdims=True)
        return jnp.sqrt(own / count + 1e-06)

    scales_a = scales_of(gram_a, rows_i * x_count * z_count)
    a_out[...] = (moved_a / scales_a).reshape(a_out.shape)

    arrived(parts_c, SCATTER_C)
    along_x_c[x] = jnp.sum(parts_c[...], axis=0)
    gather(along_x_c, x, x_peer, x_count, ALONG_X_C)
    arrived(all_moved_b, GATHER_MOVED_B)
    b_all = whole(all_moved_b)
    gram_b = dot3(b_all.T, b_all)
    arrived(along_x_c, ALONG_X_C)
    along_z_c[z] = jnp.sum(along_x_c[...], axis=0)
    gather(along_z_c, z, z_peer, z_count, ALONG_Z_C)
    scales_b = scales_of(gram_b, samples)
    b_out[...] = moved_b / scales_b
    coupled = w_pairs * gram_a * gram_b
    step = step_of(coupled)
    c_own = c_v[me]
    base = c_own - step * dot3(c_own, coupled)
    gain = step * w
    arrived(along_z_c, ALONG_Z_C)
    all_c[me] = base + gain * jnp.sum(along_z_c[...], axis=0)
    gather(all_c, me, smp_peer, s_count, GATHER_C)
    for phase, buffer in (
        (GATHER_B, all_b), (SCATTER_A, parts_a), (GATHER_A, all_a), (ALONG_X, along_x), (ALONG_Z, along_z),
        (GATHER_GRAM, all_gram), (GATHER_MOVED_B, all_moved_b), (SCATTER_C, parts_c), (ALONG_X_C, along_x_c),
        (ALONG_Z_C, along_z_c),
    ):
        arrived(buffer, phase, send_sem)
    arrived(all_c, GATHER_C)
    moved_c = whole(all_c)
    scales_c = jnp.sqrt(jnp.sum(moved_c * moved_c, axis=0, keepdims=True) / RANK + 1e-06)
    c_out[...] = (moved_c / scales_c).reshape(c_out.shape)
    w_out[...] = w * scales_a * scales_b * scales_c
    arrived(all_c, GATHER_C, send_sem)


def per_device(x_count, z_count, s_count, ensemble, voxel_factor, sample_factor, time_factor, weights):
    rows_i, rows_j, times = ensemble.shape
    f32 = jnp.float32
    chunk_i, chunk_r = rows_i // s_count, RANK // s_count
    tiles = lambda n, rows: pltpu.VMEM((n, rows, RANK), f32)
    anywhere = pl.BlockSpec(memory_space=pl.ANY)
    vmem = pl.BlockSpec(memory_space=pltpu.VMEM)
    a, b, c, w = pl.pallas_call(
        functools.partial(kernel, x_count, z_count, s_count),
        out_shape=(
            jax.ShapeDtypeStruct((rows_i, RANK), f32),
            jax.ShapeDtypeStruct((rows_j, RANK), f32),
            jax.ShapeDtypeStruct((times, RANK), f32),
            jax.ShapeDtypeStruct((1, RANK), f32),
        ),
        in_specs=[anywhere] * 5,
        out_specs=(vmem,) * 4,
        scratch_shapes=[
            pltpu.VMEM((rows_i * rows_j, times), f32),
            tiles(s_count, chunk_i), pltpu.VMEM((rows_j, RANK), f32), tiles(s_count, chunk_r), pltpu.VMEM((1, RANK), f32),
            tiles(rows_j, rows_i), pltpu.VMEM((rows_j, times, 2 * rows_i), jnp.bfloat16),
            tiles(s_count, chunk_r), tiles(s_count, chunk_i), tiles(s_count, chunk_r),
            tiles(s_count, rows_j), tiles(s_count, chunk_i), tiles(s_count, chunk_i),
            tiles(x_count, chunk_r + rows_j), tiles(z_count, chunk_r + rows_j), tiles(s_count, chunk_r),
            tiles(s_count, rows_j), tiles(s_count, chunk_r), tiles(x_count, chunk_r), tiles(z_count, chunk_r),
            tiles(s_count, chunk_r),
            pltpu.SemaphoreType.DMA((5,)), pltpu.SemaphoreType.DMA((PHASES,)), pltpu.SemaphoreType.DMA((PHASES,)),
        ],
        compiler_params=pltpu.CompilerParams(collective_id=0, has_side_effects=True),
    )(
        ensemble.reshape(rows_i * rows_j, times),
        voxel_factor.reshape(s_count, chunk_i, RANK),
        sample_factor,
        time_factor.reshape(s_count, chunk_r, RANK),
        weights.reshape(1, RANK),
    )
    return a, b, c, w.reshape(RANK)


def solution(mesh):
    vox_count, s_count = mesh.shape["vox"], mesh.shape["smp"]
    x_count = X_CHIPS
    return jax.shard_map(
        functools.partial(per_device, x_count, vox_count // x_count, s_count),
        mesh=mesh,
        in_specs=(P("vox", "smp", None), P("vox", None), P("smp", None), P(), P()),
        out_specs=(P("vox", None), P("smp", None), P(), P()),
        check_vma=False,
    )
```

```python
import functools

import jax
import jax.numpy as jnp
from jax import lax
from jax.experimental import pallas as pl
from jax.experimental.pallas import tpu as pltpu
from jax.sharding import PartitionSpec as P

MESH = pl.DeviceIdType.MESH
RANK = 128
X_CHIPS = 4

PAIR_A, LINE_A, MOVED_A, LINE_B, PAIR_B, GRAM_SCATTER, GRAM_Z, GRAM_GATHER = range(8)
TERMS_X, TERMS_Z, LINE_MOVED_B, PAIR_MOVED_B, TIME_SCATTER, TIME_Y, TIME_Z, TIME_GATHER = range(8, 16)
EXCHANGES = 16


def split(value):
    high = value.astype(jnp.bfloat16)
    low = (value - high.astype(jnp.float32)).astype(jnp.bfloat16)
    return high, low


def left_operand(value):
    return jnp.concatenate(split(value), axis=1)


def right_operand(value):
    high, low = split(value)
    return jnp.concatenate(
        [jnp.concatenate([high, low], axis=1), jnp.concatenate([high, jnp.zeros_like(low)], axis=1)], axis=0
    )


def dot_split(left, right):
    both = jnp.dot(left, right, preferred_element_type=jnp.float32)
    half = both.shape[1] // 2
    return both[:, :half] + both[:, half:]


def dot3(left, right):
    return dot_split(left_operand(left), right_operand(right))


def step_of(coupled):
    sums = jnp.sum(jnp.abs(coupled), axis=0, keepdims=True)
    return 1.0 / jnp.max(sums, axis=1, keepdims=True)


def kernel(
    x_count, y_count, z_count,
    e_in, a_in, b_in, c_in, w_in,
    a_out, b_out, c_out, w_out,
    e_v, a_v, b_v, c_v, w_v,
    contracted, e_turned,
    part_a, pair_a, line_a, moved_halves, line_b,
    gram_part, gram_got, gram_z, gram_all, terms_x, terms_z,
    line_moved_b, time_part, time_got, time_y, time_z, time_all,
    load_sem, send_sem, recv_sem,
):
    vox = lax.axis_index("vox")
    smp = lax.axis_index("smp")
    x = vox // z_count
    z = vox % z_count
    y = smp // 2
    core = smp % 2
    block_count = 2 * x_count
    block = 2 * x + core
    rows_i = a_v.shape[0] * a_v.shape[1]
    rows_j = b_v.shape[0]

    loads = [
        pltpu.make_async_copy(src, dst, load_sem.at[n])
        for n, (src, dst) in enumerate(((c_in, c_v), (b_in, b_v), (e_in, e_v), (w_in, w_v), (a_in, a_v)))
    ]
    for load in loads:
        load.start()

    partner = {"smp": 2 * y + 1 - core}

    def y_peer(d):
        return {"smp": 2 * lax.rem(y + d, y_count) + core}

    def z_peer(d):
        return {"vox": x * z_count + lax.rem(z + d, z_count)}

    def x_peer(d):
        return {"vox": lax.rem(x + d, x_count) * z_count + z}

    def block_peer(d):
        other = lax.rem(block + d, block_count)
        return {"vox": (other // 2) * z_count + z, "smp": 2 * y + other % 2}

    barrier = pltpu.get_barrier_semaphore()
    greeted = [y_peer(d) for d in range(1, y_count)] + [z_peer(d) for d in range(1, z_count)]
    greeted += [block_peer(d) for d in range(1, block_count)]
    for peer in greeted:
        pl.semaphore_signal(barrier, inc=1, device_id=peer, device_id_type=MESH)

    def copy(src, dst, exchange, device):
        pltpu.make_async_remote_copy(
            src_ref=src, dst_ref=dst, send_sem=send_sem.at[exchange], recv_sem=recv_sem.at[exchange],
            device_id=device, device_id_type=MESH,
        ).start()

    def gather(buffer, index, peer, exchange):
        for d in range(1, buffer.shape[0]):
            copy(buffer.at[index], buffer.at[index], exchange, peer(d))

    def scatter(source, buffer, exchange):
        for d in range(1, block_count):
            copy(source.at[lax.rem(block + d, block_count)], buffer.at[block], exchange, block_peer(d))
        buffer[block] = source[block]

    def take(ref, exchange, sem=recv_sem):
        pltpu.make_async_copy(ref, ref, sem.at[exchange]).wait()

    def others(buffer):
        return buffer.at[pl.ds(0, buffer.shape[0] - 1)]

    def whole(buffer):
        return buffer[...].reshape(-1, RANK)

    loads[0].wait()
    c = whole(c_v)
    c_right = right_operand(c)
    loads[1].wait()
    loads[2].wait()
    total = jnp.zeros((rows_i, RANK), jnp.float32)
    for j in range(rows_j):
        product = dot_split(left_operand(e_v[pl.ds(j, rows_i, stride=rows_j), :]), c_right)
        contracted[j] = product
        total = total + product * b_v[j : j + 1, :]
    part_a[...] = total.reshape(part_a.shape)
    line_b[core, y] = b_v[...]

    pl.semaphore_wait(barrier, len(greeted))
    copy(part_a.at[1 - core], pair_a, PAIR_A, partner)
    gather_line(copy, line_b, core, y, y_count, y_peer, LINE_B)
    take(pair_a, PAIR_A)
    line_a[y] = part_a[core] + pair_a[...]
    gather(line_a, y, y_peer, LINE_A)

    loads[3].wait()
    loads[4].wait()
    w = w_v[...]
    w_pairs = jnp.broadcast_to(w, (RANK, RANK)).T * w
    w_gram_c = w_pairs * dot3(c.T, c)
    take(line_b.at[0, pl.ds(0, y_count - 1)], LINE_B)
    copy(line_b.at[core], line_b.at[core], PAIR_B, partner)
    for j in range(rows_j):
        e_turned[j] = left_operand(e_v[pl.ds(j, rows_i, stride=rows_j), :].T)
    take(line_b.at[0], PAIR_B)
    b_all = whole(line_b)
    samples = b_all.shape[0]
    coupled = w_gram_c * dot3(b_all.T, b_all)
    step = step_of(coupled)
    a_own = a_v[core]
    base = a_own - step * dot3(a_own, coupled)
    gain = step * w
    take(others(line_a), LINE_A)
    moved = base + gain * jnp.sum(line_a[...], axis=0)

    moved_halves[core] = moved
    copy(moved_halves.at[core], moved_halves.at[core], MOVED_A, partner)
    gram_part[...] = dot3(moved.T, moved).reshape(gram_part.shape)
    scatter(gram_part, gram_got, GRAM_SCATTER)
    take(moved_halves.at[0], MOVED_A)
    moved_a = whole(moved_halves)
    terms_x[x] = jnp.concatenate(
        [jnp.sum(contracted[j] * moved_a, axis=0, keepdims=True) for j in range(rows_j)], axis=0
    )
    gather(terms_x, x, x_peer, TERMS_X)
    a_right = right_operand(moved_a)
    take(others(gram_got), GRAM_SCATTER)
    gram_z[z] = jnp.sum(gram_got[...], axis=0)
    gather(gram_z, z, z_peer, GRAM_Z)
    take(others(terms_x), TERMS_X)
    terms_z[z] = jnp.sum(terms_x[...], axis=0)
    gather(terms_z, z, z_peer, TERMS_Z)
    for j in range(rows_j):
        contracted[j] = dot_split(e_turned[j], a_right)
    b_own = b_v[...]
    b_left = left_operand(b_own)
    take(others(gram_z), GRAM_Z)
    gram_all[block] = jnp.sum(gram_z[...], axis=0)
    gather(gram_all, block, block_peer, GRAM_GATHER)
    take(others(terms_z), TERMS_Z)
    terms_b = jnp.sum(terms_z[...], axis=0) * w
    take(others(gram_all), GRAM_GATHER)

    gram_a = whole(gram_all)
    coupled = w_gram_c * gram_a
    step = step_of(coupled)
    moved_b = b_own - step * (dot_split(b_left, right_operand(coupled)) - terms_b)
    total = contracted[0] * moved_b[0:1, :]
    for j in range(1, rows_j):
        total = total + contracted[j] * moved_b[j : j + 1, :]
    time_part[...] = total.reshape(time_part.shape)
    scatter(time_part, time_got, TIME_SCATTER)
    line_moved_b[core, y] = moved_b
    gather_line(copy, line_moved_b, core, y, y_count, y_peer, LINE_MOVED_B)

    diagonal = (
        lax.broadcasted_iota(jnp.int32, (RANK, RANK), 0) == lax.broadcasted_iota(jnp.int32, (RANK, RANK), 1)
    )

    def scales_of(gram, count):
        own = jnp.sum(jnp.where(diagonal, gram, 0.0), axis=0, keepdims=True)
        return jnp.sqrt(own / count + 1e-06)

    scales_a = scales_of(gram_a, rows_i * x_count * z_count)
    a_out[...] = moved_a / scales_a
    take(others(time_got), TIME_SCATTER)
    time_y[y] = jnp.sum(time_got[...], axis=0)
    gather(time_y, y, y_peer, TIME_Y)
    take(line_moved_b.at[0, pl.ds(0, y_count - 1)], LINE_MOVED_B)
    copy(line_moved_b.at[core], line_moved_b.at[core], PAIR_MOVED_B, partner)
    take(others(time_y), TIME_Y)
    time_z[z] = jnp.sum(time_y[...], axis=0)
    gather(time_z, z, z_peer, TIME_Z)
    take(line_moved_b.at[0], PAIR_MOVED_B)
    b_all = whole(line_moved_b)
    gram_b = dot3(b_all.T, b_all)
    scales_b = scales_of(gram_b, samples)
    b_out[...] = moved_b / scales_b
    coupled = w_pairs * gram_a * gram_b
    step = step_of(coupled)
    c_own = c_v[block]
    base = c_own - step * dot3(c_own, coupled)
    gain = step * w
    scales_ab = w * scales_a * scales_b
    take(others(time_z), TIME_Z)
    time_all[block] = base + gain * jnp.sum(time_z[...], axis=0)
    gather(time_all, block, block_peer, TIME_GATHER)
    for exchange, ref in (
        (PAIR_A, pair_a), (LINE_A, others(line_a)), (MOVED_A, moved_halves.at[0]),
        (LINE_B, line_b.at[0, pl.ds(0, y_count - 1)]), (PAIR_B, line_b.at[0]),
        (GRAM_SCATTER, others(gram_got)), (GRAM_Z, others(gram_z)), (GRAM_GATHER, others(gram_all)),
        (TERMS_X, others(terms_x)), (TERMS_Z, others(terms_z)),
        (LINE_MOVED_B, line_moved_b.at[0, pl.ds(0, y_count - 1)]), (PAIR_MOVED_B, line_moved_b.at[0]),
        (TIME_SCATTER, others(time_got)), (TIME_Y, others(time_y)), (TIME_Z, others(time_z)),
    ):
        take(ref, exchange, send_sem)
    take(others(time_all), TIME_GATHER)
    moved_c = whole(time_all)
    scales_c = jnp.sqrt(jnp.sum(moved_c * moved_c, axis=0, keepdims=True) / RANK + 1e-06)
    c_out[...] = moved_c / scales_c
    w_out[...] = scales_ab * scales_c
    take(others(time_all), TIME_GATHER, send_sem)


def gather_line(copy, buffer, core, y, y_count, y_peer, exchange):
    for d in range(1, y_count):
        copy(buffer.at[core, y], buffer.at[core, y], exchange, y_peer(d))


def store(*refs):
    count = (len(refs) - 1) // 2
    copies = [pltpu.make_async_copy(refs[n], refs[count + n], refs[-1].at[n]) for n in range(count)]
    for one in copies:
        one.start()
    for one in copies:
        one.wait()


def per_device(x_count, y_count, z_count, ensemble, voxel_factor, sample_factor, time_factor, weights):
    rows_i, rows_j, times = ensemble.shape
    f32 = jnp.float32
    half, blocks = rows_i // 2, 2 * x_count
    rows = RANK // blocks
    tiles = lambda *shape: pltpu.VMEM((*shape, RANK), f32)
    hbm = pl.BlockSpec(memory_space=pltpu.HBM)
    vmem = pl.BlockSpec(memory_space=pltpu.VMEM)
    shapes = tuple(jax.ShapeDtypeStruct((n, RANK), f32) for n in (rows_i, rows_j, times, 1))
    results = pl.pallas_call(
        functools.partial(kernel, x_count, y_count, z_count),
        out_shape=shapes,
        in_specs=[hbm] * 5,
        out_specs=(vmem,) * 4,
        scratch_shapes=[
            tiles(rows_i * rows_j), tiles(2, half), tiles(rows_j), tiles(blocks, rows), tiles(1),
            tiles(rows_j, rows_i), pltpu.VMEM((rows_j, times, 2 * rows_i), jnp.bfloat16),
            tiles(2, half), tiles(half), tiles(y_count, half), tiles(2, half), tiles(2, y_count, rows_j),
            tiles(blocks, rows), tiles(blocks, rows), tiles(z_count, rows), tiles(blocks, rows),
            tiles(x_count, rows_j), tiles(z_count, rows_j),
            tiles(2, y_count, rows_j), tiles(blocks, rows), tiles(blocks, rows), tiles(y_count, rows),
            tiles(z_count, rows), tiles(blocks, rows),
            pltpu.SemaphoreType.DMA((5,)), pltpu.SemaphoreType.DMA((EXCHANGES,)), pltpu.SemaphoreType.DMA((EXCHANGES,)),
        ],
        compiler_params=pltpu.CompilerParams(collective_id=0, has_side_effects=True, vmem_limit_bytes=16 << 20),
    )(*(pltpu.with_memory_space_constraint(value, pltpu.HBM) for value in (
        ensemble.reshape(rows_i * rows_j, times),
        voxel_factor.reshape(2, half, RANK),
        sample_factor,
        time_factor.reshape(blocks, rows, RANK),
        weights.reshape(1, RANK),
    )))
    a, b, c, w = pl.pallas_call(
        store,
        out_shape=shapes,
        in_specs=[vmem] * 4,
        out_specs=(hbm,) * 4,
        scratch_shapes=[pltpu.SemaphoreType.DMA((4,))],
        compiler_params=pltpu.CompilerParams(vmem_limit_bytes=1 << 20),
    )(*results)
    return a, b, c, w.reshape(RANK)


def solution(mesh):
    vox_count, y_count = mesh.shape["vox"], mesh.shape["smp"] // 2
    x_count = X_CHIPS
    return jax.shard_map(
        functools.partial(per_device, x_count, y_count, vox_count // x_count),
        mesh=mesh,
        in_specs=(P("vox", "smp", None), P("vox", None), P("smp", None), P(), P()),
        out_specs=(P("vox", None), P("smp", None), P(), P()),
        check_vma=False,
    )
```

```python
import functools

import jax
import jax.numpy as jnp
from jax import lax
from jax.experimental import pallas as pl
from jax.experimental.pallas import tpu as pltpu
from jax.sharding import PartitionSpec as P

MESH = pl.DeviceIdType.MESH
RANK = 128
X_CHIPS = 4

PAIR_A, LINE_A, MOVED_A, LINE_B, PAIR_B, GRAM_SCATTER, GRAM_Z, GRAM_GATHER = range(8)
TERMS_X, TERMS_Z, TERMS_PAIR, STRIPS, LINE_FIXED, LINE_STEP = range(8, 14)
LINE_MOVED_B, PAIR_MOVED_B, TIME_Z, TIME_GATHER = range(14, 18)
EXCHANGES = 18


def split(value):
    high = value.astype(jnp.bfloat16)
    low = (value - high.astype(jnp.float32)).astype(jnp.bfloat16)
    return high, low


def left_operand(value):
    return jnp.concatenate(split(value), axis=1)


def right_operand(value):
    high, low = split(value)
    return jnp.concatenate(
        [jnp.concatenate([high, low], axis=1), jnp.concatenate([high, jnp.zeros_like(low)], axis=1)], axis=0
    )


def dot_split(left, right):
    both = jnp.dot(left, right, preferred_element_type=jnp.float32)
    half = both.shape[1] // 2
    return both[:, :half] + both[:, half:]


def dot3(left, right):
    return dot_split(left_operand(left), right_operand(right))


def step_of(coupled):
    sums = jnp.sum(jnp.abs(coupled), axis=0, keepdims=True)
    return 1.0 / jnp.max(sums, axis=1, keepdims=True)


def kernel(
    x_count, y_count, z_count,
    e_in, a_in, b_in, c_in, w_in,
    a_out, b_out, c_out, w_out,
    e_v, a_v, b_v, c_v, w_v,
    contracted, e_right,
    part_a, pair_a, line_a, moved_halves, line_b,
    gram_part, gram_got, gram_z, gram_all, terms_x, terms_z, terms_pair,
    strips, strips_got, strip_terms, by_rank, w_gram_c_v, w_turned, base_v,
    fixed_line, step_line,
    line_moved_b, time_z, time_all,
    load_sem, send_sem, recv_sem,
):
    vox = lax.axis_index("vox")
    smp = lax.axis_index("smp")
    x = vox // z_count
    z = vox % z_count
    y = smp // 2
    core = smp % 2
    block_count = 2 * x_count
    block = 2 * x + core
    strip = RANK // block_count
    rows_i = a_v.shape[0] * a_v.shape[1]
    rows_j = b_v.shape[0]

    loads = [
        pltpu.make_async_copy(src, dst, load_sem.at[n])
        for n, (src, dst) in enumerate(((c_in, c_v), (b_in, b_v), (e_in, e_v), (w_in, w_v), (a_in, a_v)))
    ]
    for load in loads:
        load.start()

    partner = {"smp": 2 * y + 1 - core}

    def y_peer(d):
        return {"smp": 2 * lax.rem(y + d, y_count) + core}

    def z_peer(d):
        return {"vox": x * z_count + lax.rem(z + d, z_count)}

    def x_peer(d):
        return {"vox": lax.rem(x + d, x_count) * z_count + z}

    def block_peer(d):
        other = lax.rem(block + d, block_count)
        return {"vox": (other // 2) * z_count + z, "smp": 2 * y + other % 2}

    barrier = pltpu.get_barrier_semaphore()
    greeted = [y_peer(d) for d in range(1, y_count)] + [z_peer(d) for d in range(1, z_count)]
    greeted += [block_peer(d) for d in range(1, block_count)]
    for peer in greeted:
        pl.semaphore_signal(barrier, inc=1, device_id=peer, device_id_type=MESH)

    def copy(src, dst, exchange, device):
        pltpu.make_async_remote_copy(
            src_ref=src, dst_ref=dst, send_sem=send_sem.at[exchange], recv_sem=recv_sem.at[exchange],
            device_id=device, device_id_type=MESH,
        ).start()

    def gather(buffer, index, peer, exchange):
        for d in range(1, buffer.shape[0]):
            copy(buffer.at[index], buffer.at[index], exchange, peer(d))

    def scatter(source, buffer, exchange):
        for d in range(1, block_count):
            copy(source.at[lax.rem(block + d, block_count)], buffer.at[block], exchange, block_peer(d))
        buffer[block] = source[block]

    def take(ref, exchange, sem=recv_sem):
        pltpu.make_async_copy(ref, ref, sem.at[exchange]).wait()

    def others(buffer):
        return buffer.at[pl.ds(0, buffer.shape[0] - 1)]

    def whole(buffer):
        return buffer[...].reshape(-1, RANK)

    loads[0].wait()
    c = whole(c_v)
    c_right = right_operand(c)
    loads[1].wait()
    loads[2].wait()
    total = jnp.zeros((rows_i, RANK), jnp.float32)
    for j in range(rows_j):
        product = dot_split(left_operand(e_v[pl.ds(j, rows_i, stride=rows_j), :]), c_right)
        contracted[j] = product
        total = total + product * b_v[j : j + 1, :]
    part_a[...] = total.reshape(part_a.shape)
    line_b[core, y] = b_v[...]

    pl.semaphore_wait(barrier, len(greeted))
    copy(part_a.at[1 - core], pair_a, PAIR_A, partner)
    gather_line(copy, line_b, core, y, y_count, y_peer, LINE_B)
    take(pair_a, PAIR_A)
    line_a[y] = part_a[core] + pair_a[...]
    gather(line_a, y, y_peer, LINE_A)

    loads[3].wait()
    loads[4].wait()
    w = w_v[...]
    w_columns = jnp.broadcast_to(w, (RANK, RANK)).T
    w_turned[...] = w_columns.reshape(w_turned.shape)
    w_pairs = w_columns * w
    w_gram_c = w_pairs * dot3(c.T, c)
    w_gram_c_v[...] = w_gram_c.reshape(w_gram_c_v.shape)
    b_own = b_v[...]
    b_left = left_operand(b_own)

    def turn(own, partners):
        filler = jnp.zeros((RANK - 2 * rows_j, RANK), jnp.float32)
        return jnp.concatenate([own, partners, filler], axis=0).T

    take(line_b.at[0, pl.ds(0, y_count - 1)], LINE_B)
    copy(line_b.at[core], line_b.at[core], PAIR_B, partner)
    for j in range(rows_j):
        e_right[j] = right_operand(e_v[pl.ds(j, rows_i, stride=rows_j), :])
    take(line_b.at[0], PAIR_B)
    b_turned = turn(b_own, line_b[1 - core, y])
    b_turned_right = right_operand(b_turned)
    by_rank[0] = b_turned.reshape(by_rank.shape[1:])
    b_all = whole(line_b)
    samples = b_all.shape[0]
    coupled = w_gram_c * dot3(b_all.T, b_all)
    step = step_of(coupled)
    a_own = a_v[core]
    base = a_own - step * dot3(a_own, coupled)
    gain = step * w
    take(others(line_a), LINE_A)
    moved = base + gain * jnp.sum(line_a[...], axis=0)

    moved_halves[core] = moved
    copy(moved_halves.at[core], moved_halves.at[core], MOVED_A, partner)
    gram_part[...] = dot3(moved.T, moved).reshape(gram_part.shape)
    scatter(gram_part, gram_got, GRAM_SCATTER)
    take(moved_halves.at[0], MOVED_A)
    moved_a = whole(moved_halves)
    terms_x[x] = jnp.concatenate(
        [jnp.sum(contracted[j] * moved_a, axis=0, keepdims=True) for j in range(rows_j)], axis=0
    )
    gather(terms_x, x, x_peer, TERMS_X)

    a_left = left_operand(moved_a.T)
    for j in range(rows_j):
        strips[:, j] = dot_split(a_left, e_right[j]).reshape(block_count, strip, RANK)
    for d in range(1, block_count):
        copy(strips.at[lax.rem(block + d, block_count)], strips_got.at[d - 1], STRIPS, block_peer(d))
    take(others(gram_got), GRAM_SCATTER)
    gram_z[z] = jnp.sum(gram_got[...], axis=0)
    gather(gram_z, z, z_peer, GRAM_Z)
    take(others(terms_x), TERMS_X)
    terms_z[z] = jnp.sum(terms_x[...], axis=0)
    gather(terms_z, z, z_peer, TERMS_Z)
    take(others(terms_z), TERMS_Z)
    terms_b = jnp.sum(terms_z[...], axis=0) * w
    terms_pair[core] = terms_b
    copy(terms_pair.at[core], terms_pair.at[core], TERMS_PAIR, partner)
    take(others(gram_z), GRAM_Z)
    gram_strip = jnp.sum(gram_z[...], axis=0)
    gram_all[block] = gram_strip
    gather(gram_all, block, block_peer, GRAM_GATHER)
    take(strips_got, STRIPS)

    for j in range(rows_j):
        own, partners = strips[block, j], strips_got[0, j]
        for d in range(2, block_count):
            if d % 2:
                partners = partners + strips_got[d - 1, j]
            else:
                own = own + strips_got[d - 1, j]
        strip_terms[j] = own
        strip_terms[rows_j + j] = partners

    def mix(samples_in_lanes):
        total = strip_terms[0] * samples_in_lanes[:, 0:1]
        for j in range(1, 2 * rows_j):
            total = total + strip_terms[j] * samples_in_lanes[:, j : j + 1]
        return total

    fixed_line[y] = mix(by_rank[0, block])
    gather(fixed_line, y, y_peer, LINE_FIXED)
    take(terms_pair.at[0], TERMS_PAIR)
    by_rank[1] = turn(terms_b, terms_pair[1 - core]).reshape(by_rank.shape[1:])
    pull = dot_split(left_operand(w_gram_c_v[block] * gram_strip), b_turned_right) - by_rank[1, block]
    step_line[y] = mix(pull)
    gather(step_line, y, y_peer, LINE_STEP)

    take(others(gram_all), GRAM_GATHER)
    gram_a = whole(gram_all)
    coupled = w_gram_c * gram_a
    step_b = step_of(coupled)
    moved_b = b_own - step_b * (dot_split(b_left, right_operand(coupled)) - terms_b)
    line_moved_b[core, y] = moved_b
    gather_line(copy, line_moved_b, core, y, y_count, y_peer, LINE_MOVED_B)
    take(others(fixed_line), LINE_FIXED)
    fixed = jnp.sum(fixed_line[...], axis=0)
    take(others(step_line), LINE_STEP)
    time_z[z] = fixed - step_b * jnp.sum(step_line[...], axis=0)
    gather(time_z, z, z_peer, TIME_Z)

    diagonal = (
        lax.broadcasted_iota(jnp.int32, (RANK, RANK), 0) == lax.broadcasted_iota(jnp.int32, (RANK, RANK), 1)
    )

    def scales_of(gram, count):
        own = jnp.sum(jnp.where(diagonal, gram, 0.0), axis=0, keepdims=True)
        return jnp.sqrt(own / count + 1e-06)

    take(line_moved_b.at[0, pl.ds(0, y_count - 1)], LINE_MOVED_B)
    copy(line_moved_b.at[core], line_moved_b.at[core], PAIR_MOVED_B, partner)
    scales_a = scales_of(gram_a, rows_i * x_count * z_count)
    a_out[...] = moved_a / scales_a
    take(line_moved_b.at[0], PAIR_MOVED_B)
    b_all = whole(line_moved_b)
    gram_b = dot3(b_all.T, b_all)
    coupled = w_pairs * gram_a * gram_b
    step = step_of(coupled)
    base = c - step * dot3(c, coupled)
    base_v[...] = base.T.reshape(base_v.shape)
    gain = step * w_turned[block]
    scales_b = scales_of(gram_b, samples)
    b_out[...] = moved_b / scales_b
    scales_ab = w * scales_a * scales_b
    take(others(time_z), TIME_Z)
    time_all[block] = base_v[block] + gain * jnp.sum(time_z[...], axis=0)
    gather(time_all, block, block_peer, TIME_GATHER)
    for exchange, ref in (
        (PAIR_A, pair_a), (LINE_A, others(line_a)), (MOVED_A, moved_halves.at[0]),
        (LINE_B, line_b.at[0, pl.ds(0, y_count - 1)]), (PAIR_B, line_b.at[0]),
        (GRAM_SCATTER, others(gram_got)), (GRAM_Z, others(gram_z)), (GRAM_GATHER, others(gram_all)),
        (TERMS_X, others(terms_x)), (TERMS_Z, others(terms_z)), (TERMS_PAIR, terms_pair.at[0]),
        (STRIPS, strips_got), (LINE_FIXED, others(fixed_line)), (LINE_STEP, others(step_line)),
        (LINE_MOVED_B, line_moved_b.at[0, pl.ds(0, y_count - 1)]), (PAIR_MOVED_B, line_moved_b.at[0]),
        (TIME_Z, others(time_z)),
    ):
        take(ref, exchange, send_sem)
    take(others(time_all), TIME_GATHER)
    moved_c = whole(time_all).T
    scales_c = jnp.sqrt(jnp.sum(moved_c * moved_c, axis=0, keepdims=True) / RANK + 1e-06)
    c_out[...] = moved_c / scales_c
    w_out[...] = scales_ab * scales_c
    take(others(time_all), TIME_GATHER, send_sem)


def gather_line(copy, buffer, core, y, y_count, y_peer, exchange):
    for d in range(1, y_count):
        copy(buffer.at[core, y], buffer.at[core, y], exchange, y_peer(d))


def store(*refs):
    count = (len(refs) - 1) // 2
    copies = [pltpu.make_async_copy(refs[n], refs[count + n], refs[-1].at[n]) for n in range(count)]
    for one in copies:
        one.start()
    for one in copies:
        one.wait()


def per_device(x_count, y_count, z_count, ensemble, voxel_factor, sample_factor, time_factor, weights):
    rows_i, rows_j, times = ensemble.shape
    f32 = jnp.float32
    half, blocks = rows_i // 2, 2 * x_count
    rows = RANK // blocks
    tiles = lambda *shape: pltpu.VMEM((*shape, RANK), f32)
    hbm = pl.BlockSpec(memory_space=pltpu.HBM)
    vmem = pl.BlockSpec(memory_space=pltpu.VMEM)
    shapes = tuple(jax.ShapeDtypeStruct((n, RANK), f32) for n in (rows_i, rows_j, times, 1))
    results = pl.pallas_call(
        functools.partial(kernel, x_count, y_count, z_count),
        out_shape=shapes,
        in_specs=[hbm] * 5,
        out_specs=(vmem,) * 4,
        scratch_shapes=[
            tiles(rows_i * rows_j), tiles(2, half), tiles(rows_j), tiles(blocks, rows), tiles(1),
            tiles(rows_j, rows_i), pltpu.VMEM((rows_j, 2 * rows_i, 2 * times), jnp.bfloat16),
            tiles(2, half), tiles(half), tiles(y_count, half), tiles(2, half), tiles(2, y_count, rows_j),
            tiles(blocks, rows), tiles(blocks, rows), tiles(z_count, rows), tiles(blocks, rows),
            tiles(x_count, rows_j), tiles(z_count, rows_j), tiles(2, rows_j),
            tiles(blocks, rows_j, rows), tiles(blocks - 1, rows_j, rows), tiles(2 * rows_j, rows),
            tiles(2, blocks, rows), tiles(blocks, rows), tiles(blocks, rows), tiles(blocks, rows),
            tiles(y_count, rows), tiles(y_count, rows),
            tiles(2, y_count, rows_j), tiles(z_count, rows), tiles(blocks, rows),
            pltpu.SemaphoreType.DMA((5,)), pltpu.SemaphoreType.DMA((EXCHANGES,)), pltpu.SemaphoreType.DMA((EXCHANGES,)),
        ],
        compiler_params=pltpu.CompilerParams(collective_id=0, has_side_effects=True, vmem_limit_bytes=16 << 20),
    )(*(pltpu.with_memory_space_constraint(value, pltpu.HBM) for value in (
        ensemble.reshape(rows_i * rows_j, times),
        voxel_factor.reshape(2, half, RANK),
        sample_factor,
        time_factor.reshape(blocks, rows, RANK),
        weights.reshape(1, RANK),
    )))
    a, b, c, w = pl.pallas_call(
        store,
        out_shape=shapes,
        in_specs=[vmem] * 4,
        out_specs=(hbm,) * 4,
        scratch_shapes=[pltpu.SemaphoreType.DMA((4,))],
        compiler_params=pltpu.CompilerParams(vmem_limit_bytes=1 << 20),
    )(*results)
    return a, b, c, w.reshape(RANK)


def solution(mesh):
    vox_count, y_count = mesh.shape["vox"], mesh.shape["smp"] // 2
    x_count = X_CHIPS
    return jax.shard_map(
        functools.partial(per_device, x_count, y_count, vox_count // x_count),
        mesh=mesh,
        in_specs=(P("vox", "smp", None), P("vox", None), P("smp", None), P(), P()),
        out_specs=(P("vox", None), P("smp", None), P(), P()),
        check_vma=False,
    )
```

```python
import functools

import jax
import jax.numpy as jnp
from jax import lax
from jax.experimental import pallas as pl
from jax.experimental.pallas import tpu as pltpu
from jax.sharding import PartitionSpec as P

MESH = pl.DeviceIdType.MESH
RANK = 128
X_CHIPS = 4

PAIR_A, LINE_A, MOVED_A, LINE_B, PAIR_B, GRAM_SCATTER, GRAM_Z, GRAM_GATHER = range(8)
TERMS_SCATTER, TERMS_Z, TERMS_GATHER, FIXED_SCATTER, STRIPS, LINE_FIXED, LINE_STEP = range(8, 15)
LINE_MOVED_B, PAIR_MOVED_B, TIME_Z, TIME_GATHER = range(15, 19)
EXCHANGES = 19


def split(value):
    high = value.astype(jnp.bfloat16)
    low = (value - high.astype(jnp.float32)).astype(jnp.bfloat16)
    return high, low


def left_operand(value):
    return jnp.concatenate(split(value), axis=1)


def right_operand(value):
    high, low = split(value)
    return jnp.concatenate(
        [jnp.concatenate([high, low], axis=1), jnp.concatenate([high, jnp.zeros_like(low)], axis=1)], axis=0
    )


def dot_split(left, right):
    both = jnp.dot(left, right, preferred_element_type=jnp.float32)
    half = both.shape[1] // 2
    return both[:, :half] + both[:, half:]


def dot3(left, right):
    return dot_split(left_operand(left), right_operand(right))


def far_first(count):
    return sorted(range(1, count), key=lambda d: -min(d, count - d))


def step_of(coupled):
    sums = jnp.sum(jnp.abs(coupled), axis=0, keepdims=True)
    return 1.0 / jnp.max(sums, axis=1, keepdims=True)


def kernel(
    x_count, y_count, z_count,
    e_in, a_in, b_in, c_in, w_in,
    a_out, b_out, c_out, w_out,
    e_v, a_v, b_v, c_v, w_v,
    contracted, e_right,
    part_a, pair_a, line_a, moved_halves, line_b,
    gram_part, gram_got, gram_z, gram_all, terms_part, terms_got, terms_z, terms_all, fixed_part, fixed_got,
    strips, strips_got, w_gram_c_v, w_turned, c_turned_v, coupled_v,
    fixed_line, step_line,
    line_moved_b, time_z, time_all,
    load_sem, send_sem, recv_sem,
):
    vox = lax.axis_index("vox")
    smp = lax.axis_index("smp")
    x = vox // z_count
    z = vox % z_count
    y = smp // 2
    core = smp % 2
    block_count = 2 * x_count
    block = 2 * x + core
    strip = RANK // block_count
    rows_i = a_v.shape[0] * a_v.shape[1]
    rows_j = b_v.shape[0]

    loads = [
        pltpu.make_async_copy(src, dst, load_sem.at[n])
        for n, (src, dst) in enumerate(((e_in, e_v), (c_in, c_v), (b_in, b_v), (w_in, w_v), (a_in, a_v)))
    ]
    for load in loads:
        load.start()

    partner = {"smp": 2 * y + 1 - core}

    def y_peer(d):
        return {"smp": 2 * lax.rem(y + d, y_count) + core}

    def z_peer(d):
        return {"vox": x * z_count + lax.rem(z + d, z_count)}

    def x_peer(d):
        return {"vox": lax.rem(x + d, x_count) * z_count + z}

    def block_at(dx, flip):
        return 2 * lax.rem(x + dx, x_count) + (1 - core if flip else core)

    def block_peer(dx, flip):
        return {"vox": lax.rem(x + dx, x_count) * z_count + z, "smp": 2 * y + (1 - core if flip else core)}

    block_peers = [(dx, flip) for dx in far_first(x_count) for flip in (0, 1)] + [(0, 1)]

    barrier = pltpu.get_barrier_semaphore()
    greeted = [y_peer(d) for d in far_first(y_count)] + [z_peer(d) for d in far_first(z_count)]
    greeted += [block_peer(*at) for at in block_peers]
    for peer in greeted:
        pl.semaphore_signal(barrier, inc=1, device_id=peer, device_id_type=MESH)

    def copy(src, dst, exchange, device):
        pltpu.make_async_remote_copy(
            src_ref=src, dst_ref=dst, send_sem=send_sem.at[exchange], recv_sem=recv_sem.at[exchange],
            device_id=device, device_id_type=MESH,
        ).start()

    def gather(buffer, index, peer, exchange):
        for d in far_first(buffer.shape[0]):
            copy(buffer.at[index], buffer.at[index], exchange, peer(d))

    def gather_blocks(buffer, exchange):
        for at in block_peers:
            copy(buffer.at[block], buffer.at[block], exchange, block_peer(*at))

    def scatter(source, buffer, exchange):
        for at in block_peers:
            copy(source.at[block_at(*at)], buffer.at[block], exchange, block_peer(*at))
        buffer[block] = source[block]

    def take(ref, exchange, sem=recv_sem):
        pltpu.make_async_copy(ref, ref, sem.at[exchange]).wait()

    def others(buffer):
        return buffer.at[pl.ds(0, buffer.shape[0] - 1)]

    def whole(buffer):
        return buffer[...].reshape(-1, RANK)

    loads[1].wait()
    c = whole(c_v)
    c_right = right_operand(c)
    loads[2].wait()
    loads[0].wait()
    total = jnp.zeros((rows_i, RANK), jnp.float32)
    for j in range(rows_j):
        product = dot_split(left_operand(e_v[pl.ds(j, rows_i, stride=rows_j), :]), c_right)
        contracted[j] = product
        total = total + product * b_v[j : j + 1, :]
    part_a[...] = total.reshape(part_a.shape)
    line_b[core, y] = b_v[...]

    pl.semaphore_wait(barrier, len(greeted))
    copy(part_a.at[1 - core], pair_a, PAIR_A, partner)
    gather_line(copy, line_b, core, y, y_count, y_peer, LINE_B)
    take(pair_a, PAIR_A)
    line_a[y] = part_a[core] + pair_a[...]
    gather(line_a, y, y_peer, LINE_A)

    loads[3].wait()
    loads[4].wait()
    w = w_v[...]
    w_columns = jnp.broadcast_to(w, (RANK, RANK)).T
    w_turned[...] = w_columns.reshape(w_turned.shape)
    w_pairs = w_columns * w
    w_gram_c = w_pairs * dot3(c.T, c)
    w_gram_c_v[...] = w_gram_c.reshape(w_gram_c_v.shape)
    c_turned = c.T
    c_turned_right = right_operand(c_turned)
    c_turned_v[...] = c_turned.reshape(c_turned_v.shape)
    b_own = b_v[...]
    b_left = left_operand(b_own)

    def turn(own, partners):
        filler = jnp.zeros((RANK - 2 * rows_j, RANK), jnp.float32)
        return jnp.concatenate([own, partners, filler], axis=0).T

    take(line_b.at[0, pl.ds(0, y_count - 1)], LINE_B)
    copy(line_b.at[core], line_b.at[core], PAIR_B, partner)
    for j in range(rows_j):
        e_right[j] = right_operand(e_v[pl.ds(j, rows_i, stride=rows_j), :])
    take(line_b.at[0], PAIR_B)
    b_turned = turn(b_own, line_b[1 - core, y])
    b_turned_right = right_operand(b_turned)
    b_all = whole(line_b)
    samples = b_all.shape[0]
    coupled = w_gram_c * dot3(b_all.T, b_all)
    step = step_of(coupled)
    a_own = a_v[core]
    base = a_own - step * dot3(a_own, coupled)
    gain = step * w
    take(others(line_a), LINE_A)
    moved = base + gain * jnp.sum(line_a[...], axis=0)

    moved_halves[core] = moved
    copy(moved_halves.at[core], moved_halves.at[core], MOVED_A, partner)
    gram_part[...] = dot3(moved.T, moved).reshape(gram_part.shape)
    scatter(gram_part, gram_got, GRAM_SCATTER)
    take(moved_halves.at[0], MOVED_A)
    moved_a = whole(moved_halves)
    raw_terms = jnp.concatenate(
        [jnp.sum(contracted[j] * moved_a, axis=0, keepdims=True) for j in range(rows_j)], axis=0
    )
    filler = jnp.zeros((RANK - rows_j, RANK), jnp.float32)
    packed = pack(jnp.concatenate([raw_terms, filler], axis=0).T, strip, rows_j)
    for n in range(block_count):
        terms_part[n] = packed[n]
    for n, at in enumerate(block_peers):
        copy(terms_part.at[block_at(*at)], terms_got.at[n], TERMS_SCATTER, block_peer(*at))

    a_left = left_operand(moved_a.T)
    fixed = jnp.zeros((RANK, RANK), jnp.float32)
    for j in range(rows_j):
        product = dot_split(a_left, e_right[j])
        strips[:, j] = product.reshape(block_count, strip, RANK)
        fixed = fixed + product * b_turned[:, j : j + 1]
    fixed_part[...] = fixed.reshape(fixed_part.shape)
    scatter(fixed_part, fixed_got, FIXED_SCATTER)
    for n, at in enumerate(block_peers):
        copy(strips.at[block_at(*at)], strips_got.at[n], STRIPS, block_peer(*at))
    take(others(gram_got), GRAM_SCATTER)
    gram_z[z] = jnp.sum(gram_got[...], axis=0)
    gather(gram_z, z, z_peer, GRAM_Z)
    take(terms_got, TERMS_SCATTER)
    by_core = [terms_part[block], jnp.zeros_like(terms_part[0])]
    for n, (_, flip) in enumerate(block_peers):
        by_core[flip] = by_core[flip] + terms_got[n]
    terms_z[z] = jnp.concatenate(by_core, axis=0)
    gather(terms_z, z, z_peer, TERMS_Z)
    take(others(fixed_got), FIXED_SCATTER)
    fixed_line[y] = jnp.sum(fixed_got[...], axis=0)
    gather(fixed_line, y, y_peer, LINE_FIXED)
    take(others(gram_z), GRAM_Z)
    gram_strip = jnp.sum(gram_z[...], axis=0)
    gram_all[block] = gram_strip
    gather_blocks(gram_all, GRAM_GATHER)

    pull = dot_split(left_operand(w_gram_c_v[block] * gram_strip), b_turned_right)
    take(others(terms_z), TERMS_Z)
    terms = jnp.sum(terms_z[...], axis=0)
    terms_all[block, pl.ds(core, 1), :] = terms[0:1]
    terms_all[block, pl.ds(1 - core, 1), :] = terms[1:2]
    gather_blocks(terms_all, TERMS_GATHER)
    lanes = lax.broadcasted_iota(jnp.int32, (strip, RANK), 1)
    strip_terms = jnp.where(
        lanes < rows_j, unpack(terms[0:1], strip, rows_j, 0), unpack(terms[1:2], strip, rows_j, rows_j)
    )
    pull = pull - strip_terms * w_turned[block]
    take(strips_got, STRIPS)
    total = None
    for j in range(rows_j):
        by_core = [strips[block, j], None]
        for n, (_, flip) in enumerate(block_peers):
            got = strips_got[n, j]
            by_core[flip] = got if by_core[flip] is None else by_core[flip] + got
        term = by_core[0] * pull[:, j : j + 1] + by_core[1] * pull[:, rows_j + j : rows_j + j + 1]
        total = term if total is None else total + term
    step_line[y] = total
    gather(step_line, y, y_peer, LINE_STEP)

    take(others(terms_all), TERMS_GATHER)
    columns = [
        unpack(terms_all[n, pl.ds(core, 1), :], strip, rows_j, 0) for n in range(block_count)
    ]
    terms_b = jnp.concatenate(columns, axis=0).T[:rows_j] * w
    take(others(gram_all), GRAM_GATHER)
    gram_a = whole(gram_all)
    coupled = w_gram_c * gram_a
    step_b = step_of(coupled)
    moved_b = b_own - step_b * (dot_split(b_left, right_operand(coupled)) - terms_b)
    line_moved_b[core, y] = moved_b
    gather_line(copy, line_moved_b, core, y, y_count, y_peer, LINE_MOVED_B)
    take(others(fixed_line), LINE_FIXED)
    fixed = jnp.sum(fixed_line[...], axis=0)
    take(others(step_line), LINE_STEP)
    time_z[z] = fixed - step_b * jnp.sum(step_line[...], axis=0)
    gather(time_z, z, z_peer, TIME_Z)

    diagonal = (
        lax.broadcasted_iota(jnp.int32, (RANK, RANK), 0) == lax.broadcasted_iota(jnp.int32, (RANK, RANK), 1)
    )

    def scales_of(gram, count):
        own = jnp.sum(jnp.where(diagonal, gram, 0.0), axis=0, keepdims=True)
        return jnp.sqrt(own / count + 1e-06)

    take(line_moved_b.at[0, pl.ds(0, y_count - 1)], LINE_MOVED_B)
    copy(line_moved_b.at[core], line_moved_b.at[core], PAIR_MOVED_B, partner)
    w_gram_a = w_pairs * gram_a
    scales_a = scales_of(gram_a, rows_i * x_count * z_count)
    a_out[...] = moved_a / scales_a
    take(line_moved_b.at[0], PAIR_MOVED_B)
    b_all = whole(line_moved_b)
    gram_b = dot3(b_all.T, b_all)
    coupled = w_gram_a * gram_b
    coupled_v[...] = coupled.reshape(coupled_v.shape)
    step = step_of(coupled)
    base = c_turned_v[block] - step * dot_split(left_operand(coupled_v[block]), c_turned_right)
    gain = step * w_turned[block]
    scales_b = scales_of(gram_b, samples)
    b_out[...] = moved_b / scales_b
    scales_ab = w * scales_a * scales_b
    take(others(time_z), TIME_Z)
    time_all[block] = base + gain * jnp.sum(time_z[...], axis=0)
    gather_blocks(time_all, TIME_GATHER)
    for exchange, ref in (
        (PAIR_A, pair_a), (LINE_A, others(line_a)), (MOVED_A, moved_halves.at[0]),
        (LINE_B, line_b.at[0, pl.ds(0, y_count - 1)]), (PAIR_B, line_b.at[0]),
        (GRAM_SCATTER, others(gram_got)), (GRAM_Z, others(gram_z)), (GRAM_GATHER, others(gram_all)),
        (TERMS_SCATTER, terms_got), (TERMS_Z, others(terms_z)), (TERMS_GATHER, others(terms_all)), (FIXED_SCATTER, others(fixed_got)),
        (STRIPS, strips_got), (LINE_FIXED, others(fixed_line)), (LINE_STEP, others(step_line)),
        (LINE_MOVED_B, line_moved_b.at[0, pl.ds(0, y_count - 1)]), (PAIR_MOVED_B, line_moved_b.at[0]),
        (TIME_Z, others(time_z)),
    ):
        take(ref, exchange, send_sem)
    take(others(time_all), TIME_GATHER)
    moved_c = whole(time_all).T
    scales_c = jnp.sqrt(jnp.sum(moved_c * moved_c, axis=0, keepdims=True) / RANK + 1e-06)
    c_out[...] = moved_c / scales_c
    w_out[...] = scales_ab * scales_c
    take(others(time_all), TIME_GATHER, send_sem)


def slide(value, first, each):
    value = pltpu.roll(value, first % RANK, 1) if first % RANK else value
    row = lax.broadcasted_iota(jnp.int32, value.shape, 0)
    for bit in (1, 2, 4):
        value = jnp.where((row & bit) != 0, pltpu.roll(value, bit * each % RANK, 1), value)
    return value


def pack(columns, strip, count):
    rows = []
    for start in range(0, RANK, strip):
        row = None
        for n in range(0, strip, 8):
            tile = slide(columns[start + n : start + n + 8], n * count, count)
            part = jnp.sum(tile, axis=0, keepdims=True)
            row = part if row is None else row + part
        rows.append(row)
    return rows


def unpack(row, strip, count, lane):
    tile = jnp.broadcast_to(row, (8, RANK))
    return jnp.concatenate([slide(tile, lane - n * count, -count) for n in range(0, strip, 8)], axis=0)


def gather_line(copy, buffer, core, y, y_count, y_peer, exchange):
    for d in far_first(y_count):
        copy(buffer.at[core, y], buffer.at[core, y], exchange, y_peer(d))


def store(*refs):
    count = (len(refs) - 1) // 2
    copies = [pltpu.make_async_copy(refs[n], refs[count + n], refs[-1].at[n]) for n in range(count)]
    for one in copies:
        one.start()
    for one in copies:
        one.wait()


def per_device(x_count, y_count, z_count, ensemble, voxel_factor, sample_factor, time_factor, weights):
    rows_i, rows_j, times = ensemble.shape
    f32 = jnp.float32
    half, blocks = rows_i // 2, 2 * x_count
    rows = RANK // blocks
    tiles = lambda *shape: pltpu.VMEM((*shape, RANK), f32)
    hbm = pl.BlockSpec(memory_space=pltpu.HBM)
    vmem = pl.BlockSpec(memory_space=pltpu.VMEM)
    shapes = tuple(jax.ShapeDtypeStruct((n, RANK), f32) for n in (rows_i, rows_j, times, 1))
    results = pl.pallas_call(
        functools.partial(kernel, x_count, y_count, z_count),
        out_shape=shapes,
        in_specs=[hbm] * 5,
        out_specs=(vmem,) * 4,
        scratch_shapes=[
            tiles(rows_i * rows_j), tiles(2, half), tiles(rows_j), tiles(blocks, rows), tiles(1),
            tiles(rows_j, rows_i), pltpu.VMEM((rows_j, 2 * rows_i, 2 * times), jnp.bfloat16),
            tiles(2, half), tiles(half), tiles(y_count, half), tiles(2, half), tiles(2, y_count, rows_j),
            tiles(blocks, rows), tiles(blocks, rows), tiles(z_count, rows), tiles(blocks, rows),
            tiles(blocks, 1), tiles(blocks - 1, 1), tiles(z_count, 2), tiles(blocks, 2), tiles(blocks, rows), tiles(blocks, rows),
            tiles(blocks, rows_j, rows), tiles(blocks - 1, rows_j, rows), *[tiles(blocks, rows)] * 4,
            tiles(y_count, rows), tiles(y_count, rows),
            tiles(2, y_count, rows_j), tiles(z_count, rows), tiles(blocks, rows),
            pltpu.SemaphoreType.DMA((5,)), pltpu.SemaphoreType.DMA((EXCHANGES,)), pltpu.SemaphoreType.DMA((EXCHANGES,)),
        ],
        compiler_params=pltpu.CompilerParams(collective_id=0, has_side_effects=True, vmem_limit_bytes=16 << 20),
    )(*(pltpu.with_memory_space_constraint(value, pltpu.HBM) for value in (
        ensemble.reshape(rows_i * rows_j, times),
        voxel_factor.reshape(2, half, RANK),
        sample_factor,
        time_factor.reshape(blocks, rows, RANK),
        weights.reshape(1, RANK),
    )))
    a, b, c, w = pl.pallas_call(
        store,
        out_shape=shapes,
        in_specs=[vmem] * 4,
        out_specs=(hbm,) * 4,
        scratch_shapes=[pltpu.SemaphoreType.DMA((4,))],
        compiler_params=pltpu.CompilerParams(vmem_limit_bytes=1 << 20),
    )(*results)
    return a, b, c, w.reshape(RANK)


def solution(mesh):
    vox_count, y_count = mesh.shape["vox"], mesh.shape["smp"] // 2
    x_count = X_CHIPS
    return jax.shard_map(
        functools.partial(per_device, x_count, y_count, vox_count // x_count),
        mesh=mesh,
        in_specs=(P("vox", "smp", None), P("vox", None), P("smp", None), P(), P()),
        out_specs=(P("vox", None), P("smp", None), P(), P()),
        check_vma=False,
    )
```

```python
import functools

import jax
import jax.numpy as jnp
from jax import lax
from jax.experimental import pallas as pl
from jax.experimental.pallas import tpu as pltpu
from jax.sharding import PartitionSpec as P

MESH = pl.DeviceIdType.MESH
RANK = 128
X_CHIPS = 4

PAIR_A, LINE_A, MOVED_A, LINE_B, PAIR_B, GRAM_SCATTER, GRAM_Z, GRAM_GATHER = range(8)
TERMS_SCATTER, TERMS_Z, TERMS_GATHER, FIXED_SCATTER, STRIPS, LINE_FIXED, LINE_STEP = range(8, 15)
LINE_MOVED_B, PAIR_MOVED_B, TIME_Z, TIME_GATHER = range(15, 19)
EXCHANGES = 19


def split(value):
    high = value.astype(jnp.bfloat16)
    low = (value - high.astype(jnp.float32)).astype(jnp.bfloat16)
    return high, low


def left_operand(value):
    return jnp.concatenate(split(value), axis=1)


def right_operand(value):
    high, low = split(value)
    return jnp.concatenate(
        [jnp.concatenate([high, low], axis=1), jnp.concatenate([high, jnp.zeros_like(low)], axis=1)], axis=0
    )


def dot_split(left, right):
    both = jnp.dot(left, right, preferred_element_type=jnp.float32)
    half = both.shape[1] // 2
    return both[:, :half] + both[:, half:]


def dot3(left, right):
    return dot_split(left_operand(left), right_operand(right))


def far_first(count):
    return sorted(range(1, count), key=lambda d: -min(d, count - d))


def step_of(coupled):
    sums = jnp.sum(jnp.abs(coupled), axis=0, keepdims=True)
    return 1.0 / jnp.max(sums, axis=1, keepdims=True)


def kernel(
    x_count, y_count, z_count,
    e_in, a_in, b_in, c_in, w_in,
    a_out, b_out, c_out, w_out,
    e_v, a_v, b_v, c_v, w_v,
    contracted, e_right,
    part_a, pair_a, line_a, moved_halves, line_b,
    gram_part, gram_got, gram_z, gram_all, terms_part, terms_got, terms_z, terms_all, fixed_part, fixed_got,
    strips, strips_got, w_gram_c_v, w_turned, c_turned_v, coupled_v,
    fixed_line, step_line,
    line_moved_b, time_z, time_all,
    load_sem, send_sem, recv_sem,
):
    vox = lax.axis_index("vox")
    smp = lax.axis_index("smp")
    x = vox // z_count
    z = vox % z_count
    y = smp // 2
    core = smp % 2
    block_count = 2 * x_count
    block = 2 * x + core
    strip = RANK // block_count
    rows_i = a_v.shape[0] * a_v.shape[1]
    rows_j = b_v.shape[0]

    loads = [
        pltpu.make_async_copy(src, dst, load_sem.at[n])
        for n, (src, dst) in enumerate(((e_in, e_v), (c_in, c_v), (b_in, b_v), (w_in, w_v), (a_in, a_v)))
    ]
    for load in loads:
        load.start()

    partner = {"smp": 2 * y + 1 - core}

    def y_peer(d):
        return {"smp": 2 * lax.rem(y + d, y_count) + core}

    def z_peer(d):
        return {"vox": x * z_count + lax.rem(z + d, z_count)}

    def x_peer(d):
        return {"vox": lax.rem(x + d, x_count) * z_count + z}

    def block_at(dx, flip):
        return 2 * lax.rem(x + dx, x_count) + (1 - core if flip else core)

    def block_peer(dx, flip):
        return {"vox": lax.rem(x + dx, x_count) * z_count + z, "smp": 2 * y + (1 - core if flip else core)}

    block_peers = [(dx, flip) for dx in far_first(x_count) for flip in (0, 1)] + [(0, 1)]

    barrier = pltpu.get_barrier_semaphore()
    greeted = [y_peer(d) for d in far_first(y_count)] + [z_peer(d) for d in far_first(z_count)]
    greeted += [block_peer(*at) for at in block_peers]
    for peer in greeted:
        pl.semaphore_signal(barrier, inc=1, device_id=peer, device_id_type=MESH)

    def copy(src, dst, exchange, device):
        pltpu.make_async_remote_copy(
            src_ref=src, dst_ref=dst, send_sem=send_sem.at[exchange], recv_sem=recv_sem.at[exchange],
            device_id=device, device_id_type=MESH,
        ).start()

    def gather(buffer, index, peer, exchange):
        for d in far_first(buffer.shape[0]):
            copy(buffer.at[index], buffer.at[index], exchange, peer(d))

    def gather_blocks(buffer, exchange):
        for at in block_peers:
            copy(buffer.at[block], buffer.at[block], exchange, block_peer(*at))

    def scatter(source, buffer, exchange):
        for at in block_peers:
            copy(source.at[block_at(*at)], buffer.at[block], exchange, block_peer(*at))
        buffer[block] = source[block]

    def take(ref, exchange, sem=recv_sem):
        pltpu.make_async_copy(ref, ref, sem.at[exchange]).wait()

    def others(buffer):
        return buffer.at[pl.ds(0, buffer.shape[0] - 1)]

    def whole(buffer):
        return buffer[...].reshape(-1, RANK)

    loads[1].wait()
    c = whole(c_v)
    c_right = right_operand(c)
    loads[2].wait()
    loads[0].wait()
    half = rows_i // 2

    def voxel_terms(side):
        start = pl.multiple_of(side * half, half)
        total = jnp.zeros((half, RANK), jnp.float32)
        for j in range(rows_j):
            rows = e_v[pl.ds(start * rows_j + j, half, stride=rows_j), :]
            product = dot_split(left_operand(rows), c_right)
            contracted[j, pl.ds(start, half), :] = product
            total = total + product * b_v[j : j + 1, :]
        part_a[side] = total

    voxel_terms(1 - core)
    pl.semaphore_wait(barrier, len(greeted))
    copy(part_a.at[1 - core], pair_a, PAIR_A, partner)
    line_b[core, y] = b_v[...]
    gather_line(copy, line_b, core, y, y_count, y_peer, LINE_B)
    voxel_terms(core)
    take(pair_a, PAIR_A)
    line_a[y] = part_a[core] + pair_a[...]
    gather(line_a, y, y_peer, LINE_A)

    loads[3].wait()
    loads[4].wait()
    w = w_v[...]
    w_columns = jnp.broadcast_to(w, (RANK, RANK)).T
    w_turned[...] = w_columns.reshape(w_turned.shape)
    w_pairs = w_columns * w
    w_gram_c = w_pairs * dot3(c.T, c)
    w_gram_c_v[...] = w_gram_c.reshape(w_gram_c_v.shape)
    c_turned = c.T
    c_turned_right = right_operand(c_turned)
    c_turned_v[...] = c_turned.reshape(c_turned_v.shape)
    b_own = b_v[...]
    b_left = left_operand(b_own)

    def turn(own, partners):
        first = lax.broadcasted_iota(jnp.int32, (8, RANK), 0) == 0
        tiles = [
            jnp.where(first, rows[n : n + 1], 0.0) for n in range(rows_j) for rows in (own, partners)
        ]
        return jnp.concatenate(tiles, axis=0).T

    take(line_b.at[0, pl.ds(0, y_count - 1)], LINE_B)
    copy(line_b.at[core], line_b.at[core], PAIR_B, partner)
    for j in range(rows_j):
        e_right[j] = right_operand(e_v[pl.ds(j, rows_i, stride=rows_j), :])
    take(line_b.at[0], PAIR_B)
    b_turned = turn(b_own, line_b[1 - core, y])
    b_turned_right = right_operand(b_turned)
    b_all = whole(line_b)
    samples = b_all.shape[0]
    coupled = w_gram_c * dot3(b_all.T, b_all)
    step = step_of(coupled)
    a_own = a_v[core]
    base = a_own - step * dot3(a_own, coupled)
    gain = step * w
    take(others(line_a), LINE_A)
    moved = base + gain * jnp.sum(line_a[...], axis=0)

    moved_halves[core] = moved
    copy(moved_halves.at[core], moved_halves.at[core], MOVED_A, partner)
    gram_part[...] = dot3(moved.T, moved).reshape(gram_part.shape)
    scatter(gram_part, gram_got, GRAM_SCATTER)
    take(moved_halves.at[0], MOVED_A)
    moved_a = whole(moved_halves)
    raw_terms = jnp.concatenate(
        [jnp.sum(contracted[j] * moved_a, axis=0, keepdims=True) for j in range(rows_j)], axis=0
    )
    packed = pack(raw_terms, strip)
    for n in range(block_count):
        terms_part[n] = packed[n]
    for n, at in enumerate(block_peers):
        copy(terms_part.at[block_at(*at)], terms_got.at[n], TERMS_SCATTER, block_peer(*at))

    a_left = left_operand(moved_a.T)
    fixed = jnp.zeros((RANK, RANK), jnp.float32)
    for j in range(rows_j):
        product = dot_split(a_left, e_right[j])
        strips[:, j] = product.reshape(block_count, strip, RANK)
        fixed = fixed + product * b_turned[:, j * strip : j * strip + 1]
    fixed_part[...] = fixed.reshape(fixed_part.shape)
    scatter(fixed_part, fixed_got, FIXED_SCATTER)
    for n, at in enumerate(block_peers):
        copy(strips.at[block_at(*at)], strips_got.at[n], STRIPS, block_peer(*at))
    take(others(gram_got), GRAM_SCATTER)
    gram_z[z] = jnp.sum(gram_got[...], axis=0)
    gather(gram_z, z, z_peer, GRAM_Z)
    take(terms_got, TERMS_SCATTER)
    by_core = [terms_part[block], jnp.zeros_like(terms_part[0])]
    for n, (_, flip) in enumerate(block_peers):
        by_core[flip] = by_core[flip] + terms_got[n]
    terms_z[z] = jnp.concatenate(by_core, axis=0)
    gather(terms_z, z, z_peer, TERMS_Z)
    take(others(fixed_got), FIXED_SCATTER)
    fixed_line[y] = jnp.sum(fixed_got[...], axis=0)
    gather(fixed_line, y, y_peer, LINE_FIXED)
    take(others(gram_z), GRAM_Z)
    gram_strip = jnp.sum(gram_z[...], axis=0)
    gram_all[block] = gram_strip
    gather_blocks(gram_all, GRAM_GATHER)

    pull = dot_split(left_operand(w_gram_c_v[block] * gram_strip), b_turned_right)
    take(others(terms_z), TERMS_Z)
    terms = jnp.sum(terms_z[...], axis=0)
    lanes = lax.broadcasted_iota(jnp.int32, (strip, RANK), 1)
    strip_terms = jnp.where(lanes % strip == 0, spread(terms[0:1], strip, 0), spread(terms[1:2], strip, 8))
    pull = pull - strip_terms * w_turned[block]
    terms_all[block, pl.ds(core, 1), :] = terms[0:1]
    terms_all[block, pl.ds(1 - core, 1), :] = terms[1:2]
    gather_blocks(terms_all, TERMS_GATHER)
    take(strips_got, STRIPS)
    total = None
    for j in range(rows_j):
        by_core = [strips[block, j], None]
        for n, (_, flip) in enumerate(block_peers):
            got = strips_got[n, j]
            by_core[flip] = got if by_core[flip] is None else by_core[flip] + got
        term = by_core[0] * pull[:, j * strip : j * strip + 1] + by_core[1] * pull[:, j * strip + 8 : j * strip + 9]
        total = term if total is None else total + term
    step_line[y] = total
    gather(step_line, y, y_peer, LINE_STEP)

    take(others(terms_all), TERMS_GATHER)
    terms_b = w * unpack([terms_all[n, pl.ds(core, 1), :] for n in range(block_count)], strip)
    take(others(gram_all), GRAM_GATHER)
    gram_a = whole(gram_all)
    coupled = w_gram_c * gram_a
    step_b = step_of(coupled)
    moved_b = b_own - step_b * (dot_split(b_left, right_operand(coupled)) - terms_b)
    line_moved_b[core, y] = moved_b
    gather_line(copy, line_moved_b, core, y, y_count, y_peer, LINE_MOVED_B)
    take(others(fixed_line), LINE_FIXED)
    fixed = jnp.sum(fixed_line[...], axis=0)
    take(others(step_line), LINE_STEP)
    time_z[z] = fixed - step_b * jnp.sum(step_line[...], axis=0)
    gather(time_z, z, z_peer, TIME_Z)

    diagonal = (
        lax.broadcasted_iota(jnp.int32, (RANK, RANK), 0) == lax.broadcasted_iota(jnp.int32, (RANK, RANK), 1)
    )

    def scales_of(gram, count):
        own = jnp.sum(jnp.where(diagonal, gram, 0.0), axis=0, keepdims=True)
        return jnp.sqrt(own / count + 1e-06)

    take(line_moved_b.at[0, pl.ds(0, y_count - 1)], LINE_MOVED_B)
    copy(line_moved_b.at[core], line_moved_b.at[core], PAIR_MOVED_B, partner)
    w_gram_a = w_pairs * gram_a
    scales_a = scales_of(gram_a, rows_i * x_count * z_count)
    a_out[...] = moved_a / scales_a
    take(line_moved_b.at[0], PAIR_MOVED_B)
    b_all = whole(line_moved_b)
    gram_b = dot3(b_all.T, b_all)
    coupled = w_gram_a * gram_b
    coupled_v[...] = coupled.reshape(coupled_v.shape)
    step = step_of(coupled)
    base = c_turned_v[block] - step * dot_split(left_operand(coupled_v[block]), c_turned_right)
    gain = step * w_turned[block]
    scales_b = scales_of(gram_b, samples)
    b_out[...] = moved_b / scales_b
    scales_ab = w * scales_a * scales_b
    take(others(time_z), TIME_Z)
    time_all[block] = base + gain * jnp.sum(time_z[...], axis=0)
    gather_blocks(time_all, TIME_GATHER)
    for exchange, ref in (
        (PAIR_A, pair_a), (LINE_A, others(line_a)), (MOVED_A, moved_halves.at[0]),
        (LINE_B, line_b.at[0, pl.ds(0, y_count - 1)]), (PAIR_B, line_b.at[0]),
        (GRAM_SCATTER, others(gram_got)), (GRAM_Z, others(gram_z)), (GRAM_GATHER, others(gram_all)),
        (TERMS_SCATTER, terms_got), (TERMS_Z, others(terms_z)), (TERMS_GATHER, others(terms_all)), (FIXED_SCATTER, others(fixed_got)),
        (STRIPS, strips_got), (LINE_FIXED, others(fixed_line)), (LINE_STEP, others(step_line)),
        (LINE_MOVED_B, line_moved_b.at[0, pl.ds(0, y_count - 1)]), (PAIR_MOVED_B, line_moved_b.at[0]),
        (TIME_Z, others(time_z)),
    ):
        take(ref, exchange, send_sem)
    take(others(time_all), TIME_GATHER)
    moved_c = whole(time_all).T
    scales_c = jnp.sqrt(jnp.sum(moved_c * moved_c, axis=0, keepdims=True) / RANK + 1e-06)
    c_out[...] = moved_c / scales_c
    w_out[...] = scales_ab * scales_c
    take(others(time_all), TIME_GATHER, send_sem)


def slide(value, first, each):
    value = pltpu.roll(value, first % RANK, 1) if first % RANK else value
    row = lax.broadcasted_iota(jnp.int32, value.shape, 0)
    for bit in (1, 2, 4):
        value = jnp.where((row & bit) != 0, pltpu.roll(value, bit * each % RANK, 1), value)
    return value


def chunks(strip):
    return lax.broadcasted_iota(jnp.int32, (8, RANK), 0), lax.broadcasted_iota(jnp.int32, (8, RANK), 1) // strip


def pack(samples, strip):
    row, chunk = chunks(strip)
    moved = slide(samples, 0, strip)
    rows = []
    for n in range(RANK // strip):
        tile = pltpu.roll(moved, -n * strip % RANK, 1) if n else moved
        rows.append(jnp.sum(jnp.where(chunk == row, tile, 0.0), axis=0, keepdims=True))
    return rows


def unpack(rows, strip):
    row, chunk = chunks(strip)
    total = jnp.zeros((8, RANK), jnp.float32)
    for n, packed in enumerate(rows):
        packed = pltpu.roll(packed, n * strip % RANK, 1) if n else packed
        total = jnp.where(chunk == (row + n) % 8, jnp.broadcast_to(packed, (8, RANK)), total)
    return slide(total, 0, -strip)


def spread(packed, strip, lane):
    tile = jnp.broadcast_to(packed, (8, RANK))
    return jnp.concatenate([slide(tile, lane - n, -1) for n in range(0, strip, 8)], axis=0)


def gather_line(copy, buffer, core, y, y_count, y_peer, exchange):
    for d in far_first(y_count):
        copy(buffer.at[core, y], buffer.at[core, y], exchange, y_peer(d))


def store(*refs):
    count = (len(refs) - 1) // 2
    copies = [pltpu.make_async_copy(refs[n], refs[count + n], refs[-1].at[n]) for n in range(count)]
    for one in copies:
        one.start()
    for one in copies:
        one.wait()


def per_device(x_count, y_count, z_count, ensemble, voxel_factor, sample_factor, time_factor, weights):
    rows_i, rows_j, times = ensemble.shape
    f32 = jnp.float32
    half, blocks = rows_i // 2, 2 * x_count
    rows = RANK // blocks
    tiles = lambda *shape: pltpu.VMEM((*shape, RANK), f32)
    hbm = pl.BlockSpec(memory_space=pltpu.HBM)
    vmem = pl.BlockSpec(memory_space=pltpu.VMEM)
    shapes = tuple(jax.ShapeDtypeStruct((n, RANK), f32) for n in (rows_i, rows_j, times, 1))
    results = pl.pallas_call(
        functools.partial(kernel, x_count, y_count, z_count),
        out_shape=shapes,
        in_specs=[hbm] * 5,
        out_specs=(vmem,) * 4,
        scratch_shapes=[
            tiles(rows_i * rows_j), tiles(2, half), tiles(rows_j), tiles(blocks, rows), tiles(1),
            tiles(rows_j, rows_i), pltpu.VMEM((rows_j, 2 * rows_i, 2 * times), jnp.bfloat16),
            tiles(2, half), tiles(half), tiles(y_count, half), tiles(2, half), tiles(2, y_count, rows_j),
            tiles(blocks, rows), tiles(blocks, rows), tiles(z_count, rows), tiles(blocks, rows),
            tiles(blocks, 1), tiles(blocks - 1, 1), tiles(z_count, 2), tiles(blocks, 2), tiles(blocks, rows), tiles(blocks, rows),
            tiles(blocks, rows_j, rows), tiles(blocks - 1, rows_j, rows), *[tiles(blocks, rows)] * 4,
            tiles(y_count, rows), tiles(y_count, rows),
            tiles(2, y_count, rows_j), tiles(z_count, rows), tiles(blocks, rows),
            pltpu.SemaphoreType.DMA((5,)), pltpu.SemaphoreType.DMA((EXCHANGES,)), pltpu.SemaphoreType.DMA((EXCHANGES,)),
        ],
        compiler_params=pltpu.CompilerParams(collective_id=0, has_side_effects=True, vmem_limit_bytes=16 << 20),
    )(*(pltpu.with_memory_space_constraint(value, pltpu.HBM) for value in (
        ensemble.reshape(rows_i * rows_j, times),
        voxel_factor.reshape(2, half, RANK),
        sample_factor,
        time_factor.reshape(blocks, rows, RANK),
        weights.reshape(1, RANK),
    )))
    a, b, c, w = pl.pallas_call(
        store,
        out_shape=shapes,
        in_specs=[vmem] * 4,
        out_specs=(hbm,) * 4,
        scratch_shapes=[pltpu.SemaphoreType.DMA((4,))],
        compiler_params=pltpu.CompilerParams(vmem_limit_bytes=1 << 20),
    )(*results)
    return a, b, c, w.reshape(RANK)


def solution(mesh):
    vox_count, y_count = mesh.shape["vox"], mesh.shape["smp"] // 2
    x_count = X_CHIPS
    return jax.shard_map(
        functools.partial(per_device, x_count, y_count, vox_count // x_count),
        mesh=mesh,
        in_specs=(P("vox", "smp", None), P("vox", None), P("smp", None), P(), P()),
        out_specs=(P("vox", None), P("smp", None), P(), P()),
        check_vma=False,
    )
```
